256 devices in a mesh: pix: 64 (over z, y, core), chan: 4 (over x).
Axes of the slice: x: 4, y: 4, z: 8, core: 2. Of those that a mesh axis runs over, the one named last changes fastest.
Arguments:
- spectra: bfloat16 [262144, 2048], P('pix', 'chan'), may hold values from 0.05 to 2100, as said below
- start: bfloat16 [64, 2048], P(None, 'chan'), may hold values from -6 to 6
- anchors: int32 [16], replicated, may hold values from 0 to 262143, as said below
Outputs:
- scores: float32 [64, 262144], P(None, 'pix')
- abundance: float32 [16, 262144], P(None, 'pix')
The draws below stay inside these ranges and needn't reach their ends.
Inputs may be any that keep to these rules, and one draw needn't show every extreme that they name: `spectra`: every entry is positive. `anchors`: the 16 indices are distinct; pixel 0 and pixel 262144 - 1 are among them.
All inputs are finite; a program needn't handle non-finite values.
Results may differ from the reference program's by a relative error of at most 0.035.
Values may be sent and summed in bfloat16 or wider, within the bound.
No kernel may reach another device: no remote copies, remote signals or barrier semaphores. Data moves between devices by JAX's collectives and lax.ppermute only.
A program may use at most 64 MiB of HBM per device.

```python
import math
import jax
import jax.numpy as jnp
from jax import lax

CH = 2048
K = 64
NA = 16
ITERS = 5
PIX_DEV = 4096
PIX = 262144
N_PIX = 64
N_CHAN = 4


def draw_spectra(key, part):
    key_row, key_col, key_unit = jax.random.split(jax.random.fold_in(key, 11), 3)
    place = jnp.arange(PIX, dtype=jnp.float32) / max(PIX - 1, 1)
    energy = jnp.arange(CH, dtype=jnp.float32) / max(CH - 1, 1) - 0.5
    rise_pix = jnp.exp(math.log(3.0) * place)
    col_scale = jnp.exp(jax.random.uniform(key_col, (CH,), jnp.float32) * math.log(10.0))
    row_scale = jnp.exp(jax.random.uniform(key_row, (PIX,), jnp.float32) * math.log(10.0)) * rise_pix
    unit = jax.random.uniform(key_unit, (PIX, CH), jnp.float32, 0.25, 1.75)
    slope = math.log(8.0)
    tilt = jnp.exp(slope * place[:, None] * energy[None, :])
    values = unit * row_scale[:, None] * col_scale[None, :] * tilt
    return values.astype(jnp.bfloat16)


def draw_anchors(key, part):
    order = jax.random.permutation(jax.random.fold_in(key, 7), PIX - 2) + 1
    inner = order[:NA - 2].astype(jnp.int32)
    ends = jnp.array([0, PIX - 1], dtype=jnp.int32)
    return jnp.concatenate([ends[:1], inner, ends[1:]]).astype(jnp.int32)


def levels(stream_key, extent, cuts, least, high):
    loudness = 1.0
    for dim, blocks in cuts:
        draws = jax.random.uniform(jax.random.fold_in(jax.random.fold_in(stream_key, 6), dim), (blocks,), jnp.float32, least / len(cuts), high / len(cuts))
        loudness = loudness * jnp.repeat(jnp.exp(draws), extent[dim] // blocks).reshape((-1,) + (1,) * (len(extent) - 1 - dim))
    return loudness


def bell_draw(own_key, extent, deviation, limit, cuts=(), kind=jnp.bfloat16):
    drawn = deviation * jax.random.normal(own_key, extent, jnp.float32)
    if cuts:
        drawn = drawn * levels(own_key, extent, cuts, -0.22, 0.18)
    return jnp.clip(drawn, -limit, limit).astype(kind)


def setup_inputs(seed: int = 0) -> dict:
    splits = jax.random.split(jax.random.key(seed), 4)
    return {
        "spectra": draw_spectra(jax.random.fold_in(splits[3], 71), 0),
        "start": bell_draw(splits[1], (K, CH), 1.0, 6.0, ((1, 4),)),
        "anchors": draw_anchors(jax.random.fold_in(splits[3], 71), 0),
    }


def weigh(block, rowsum, colsum, total):
    expect = rowsum[:, None] * colsum[None, :] / total
    return ((block.astype(jnp.float32) - expect) * lax.rsqrt(expect)).astype(jnp.bfloat16)

def tri_solve(lower, rhs):
    return lax.linalg.triangular_solve(lower, rhs, left_side=True, lower=True)

def reference(spectra, start, anchors):
    rowsum = lax.optimization_barrier(jnp.sum(spectra, axis=1, dtype=jnp.float32))
    colsum = lax.optimization_barrier(jnp.sum(spectra, axis=0, dtype=jnp.float32))
    total = jnp.sum(colsum)
    blocks = spectra.reshape(N_PIX, PIX_DEV, CH)
    row_blocks = rowsum.reshape(N_PIX, PIX_DEV)
    group = CH // N_CHAN
    loadings = start
    for step in range(ITERS):

        def visit(acc, item):
            block, rows_here = item
            weighted = weigh(block, rows_here, colsum, total)
            summed = jnp.zeros((K, PIX_DEV), jnp.float32)
            for g in range(N_CHAN):
                part = jnp.dot(loadings[:, g * group:(g + 1) * group].astype(jnp.float32), weighted[:, g * group:(g + 1) * group].T.astype(jnp.float32), preferred_element_type=jnp.float32)
                summed = summed + part.astype(jnp.bfloat16).astype(jnp.float32)
            proj = summed.astype(jnp.bfloat16)
            return (acc + jnp.dot(proj.astype(jnp.float32), weighted.astype(jnp.float32), preferred_element_type=jnp.float32), None)
        back, unused = lax.scan(visit, jnp.zeros((K, CH), jnp.float32), (blocks, row_blocks))
        gram = jnp.dot(back, back.T, precision=lax.Precision.HIGHEST)
        lower = jnp.linalg.cholesky(gram)
        loadings = tri_solve(lower, back).astype(jnp.bfloat16)

    def score_block(item):
        block, rows_here = item
        weighted = weigh(block, rows_here, colsum, total)
        return jnp.dot(loadings.astype(jnp.float32), weighted.T.astype(jnp.float32), preferred_element_type=jnp.float32)
    scores = lax.map(score_block, (blocks, row_blocks))
    scores = jnp.transpose(scores, (1, 0, 2)).reshape(K, PIX)
    rows = scores[:, anchors.astype(jnp.int32)].T
    small = jnp.dot(rows, rows.T, precision=lax.Precision.HIGHEST)
    lower = jnp.linalg.cholesky(small)
    rhs = jnp.dot(rows, scores, precision=lax.Precision.HIGHEST)
    middle = tri_solve(lower, rhs)
    abundance = lax.linalg.triangular_solve(lower, middle, left_side=True, lower=True, transpose_a=True)
    return (scores, abundance)
```

```python
import jax
import jax.numpy as jnp
from jax import lax
from jax.sharding import Mesh, PartitionSpec as P

ITERS = 5
NZ, NY, NC, NX = 8, 4, 2, 4
F32, BF16 = jnp.float32, jnp.bfloat16
HIGHEST = lax.Precision.HIGHEST


def tri_solve(lower, rhs, **kw):
    return lax.linalg.triangular_solve(lower, rhs, left_side=True, lower=True, **kw)


def ring(n, step):
    return [(i, (i + step) % n) for i in range(n)]


def from_x(v, d):
    return lax.ppermute(v, "x", ring(NX, -d))


def tn(a, b):
    return lax.dot_general(a, b, (((0,), (0,)), ((), ())), preferred_element_type=F32)


def nt(a, b, **kw):
    return lax.dot_general(a, b, (((1,), (1,)), ((), ())), preferred_element_type=F32, **kw)


def pair_sum(a, b, c, d):
    return (a + b) + (c + d)


def weigh(block, rowsum, colsum, total):
    expect = rowsum[:, None] * colsum[None, :] / total
    return ((block.astype(F32) - expect) * lax.rsqrt(expect)).astype(BF16)


def in_order(parts, me):
    n = len(parts)
    twice = jnp.stack(parts + parts[:-1])
    return lax.dynamic_slice_in_dim(twice, (n - me) % n, n, 0)


def local(spectra, start, anchors):
    pix, grp = spectra.shape
    k = start.shape[0]
    na = anchors.shape[0]
    x, core, y, z = (lax.axis_index(a) for a in ("x", "core", "y", "z"))
    quart = pix // NX

    def quarter(v, j):
        return lax.dynamic_slice_in_dim(v, ((j + 2 * NX) % NX) * quart, quart, 0)

    first = core == 0
    up_a = lax.ppermute(quarter(spectra, x - 2), "x", ring(NX, -1))
    dn_a = lax.ppermute(quarter(spectra, x), "x", ring(NX, 1))
    up_b = lax.ppermute(quarter(spectra, x - 1), "x", ring(NX, -1))
    dn_b = lax.ppermute(quarter(spectra, x + 1), "x", ring(NX, 1))
    pairs = [(i, (i - 1) % NX) for i in range(NX)] + [(NX + i, NX + (i + 1) % NX) for i in range(NX)]
    extra = lax.ppermute(quarter(spectra, jnp.where(first, x + 1, x + 2)), ("core", "x"), pairs)

    col_part = jnp.sum(spectra, axis=0, dtype=F32)
    row_part = jnp.sum(spectra, axis=1, dtype=F32)
    rowsum = pair_sum(row_part, from_x(row_part, 2), from_x(row_part, 1), from_x(row_part, 3))
    npix = NZ * NY * NC
    every = lax.all_to_all(jnp.broadcast_to(col_part[None], (npix, grp)), ("z", "y", "core"), 0, 0, tiled=True)
    col = [jnp.sum(every, axis=0)]
    col += [from_x(col[0], d) for d in (1, 2, 3)]
    sums = [jnp.sum(v) for v in col]
    total = pair_sum(sums[0], sums[2], sums[1], sums[3])

    w = weigh(spectra, rowsum, col[0], total)
    quarter_rows = lambda j: quarter(rowsum, j)
    w_up = weigh(jnp.concatenate([up_a, up_b]), jnp.concatenate([quarter_rows(x - 1), quarter_rows(x)]), col[1], total)
    w_dn = weigh(jnp.concatenate([dn_a, dn_b]), jnp.concatenate([quarter_rows(x - 1), quarter_rows(x)]), col[3], total)
    j_extra = jnp.where(first, x - 2, x + 1)
    w_ex = weigh(extra, quarter_rows(j_extra), jnp.where(first, col[1], col[3]), total)

    own_a, own_b, own_ex = quarter(w, x - 1), quarter(w, x), quarter(w, j_extra)
    g_own = tn(w, w)
    g_up = tn(own_a, w_up[:quart])
    g_dn = tn(w_dn, jnp.concatenate([own_a, own_b]))
    swap = (x == 0) | (x == 3)
    g_op = tn(jnp.where(swap, w_up, w_dn), jnp.where(swap, w_dn, w_up))
    g_ex = tn(jnp.where(first, own_ex, w_ex), jnp.where(first, w_ex, own_ex))
    g_up = g_up + jnp.where(first, g_ex, 0.0)
    g_dn = g_dn + jnp.where(first, 0.0, g_ex)
    g = jnp.stack([g_own, g_up, g_dn, g_op])

    offset = ((z * NY + y) * NC + core) * pix
    positions = lax.broadcasted_iota(jnp.int32, (na, pix), 1)
    picks = (anchors[:, None] - offset == positions).astype(BF16)
    picked = jnp.dot(picks, w, preferred_element_type=F32)
    share = lax.all_to_all(picked.reshape(npix, na * grp // npix), ("z", "y", "core"), 0, 0, tiled=True)
    share = jnp.sum(share, axis=0)
    held = lax.all_to_all(jnp.broadcast_to(share[None], (npix, share.shape[0])), ("z", "y", "core"), 0, 0, tiled=True)
    anchor_w = held.reshape(na, grp).astype(BF16)
    anchor_ws = [anchor_w] + [from_x(anchor_w, d) for d in (1, 2, 3)]

    n1, n2, n3 = grp // NC, grp // NC // NY, grp // npix
    take = lambda v, i, n: lax.dynamic_slice_in_dim(v, i * n, n, 1)
    g = take(g, core, n1) + lax.ppermute(take(g, 1 - core, n1), "core", ring(NC, 1))
    sent = [lax.ppermute(take(g, (y + d) % NY, n2), "y", ring(NY, d)) for d in (1, 2, 3)]
    g = take(g, y, n2) + sent[0] + sent[1] + sent[2]
    g = g.reshape(4, NZ, n3, grp).transpose(1, 0, 2, 3)
    g = jnp.sum(lax.all_to_all(g, "z", 0, 0, tiled=True), axis=0)
    below = lax.ppermute(jnp.stack([g[1], g[3]]), "x", ring(NX, 1))
    above = lax.ppermute(jnp.stack([g[2], g[3]]), "x", ring(NX, -1))
    g = jnp.stack([g[0], g[1] + above[0], g[2] + below[0], below[1] + above[1]])
    g = lax.all_to_all(jnp.broadcast_to(g[None], (NZ,) + g.shape), "z", 0, 0, tiled=True)
    g = in_order([g] + [lax.ppermute(g, "y", ring(NY, -d)) for d in (1, 2, 3)], y)
    g = in_order([g, lax.ppermute(g, "core", ring(NC, 1))], core)
    g = g.transpose(3, 0, 1, 2, 4, 5).reshape(4, grp, grp)
    opposite = jnp.where(x < 2, g[3].T, g[3])
    g = jnp.concatenate([g[0], g[1].T, opposite, g[2]])
    rounded = lax.reduce_precision(g, 8, 7)
    g_hi, g_lo = rounded.astype(BF16), (g - rounded).astype(BF16)

    loads = [start] + [from_x(start, d) for d in (1, 2, 3)]
    for step in range(ITERS):
        whole = jnp.concatenate(loads, axis=1)
        back = jnp.dot(whole, g_hi, preferred_element_type=F32) + jnp.dot(whole, g_lo, preferred_element_type=F32)
        backs = [back] + [from_x(back, d) for d in (1, 2, 3)]
        grams = [nt(b, b, precision=HIGHEST) for b in backs]
        gram = pair_sum(grams[0], grams[2], grams[1], grams[3])
        lower = jnp.linalg.cholesky(gram)
        loads = [v.astype(BF16) for v in jnp.split(tri_solve(lower, jnp.concatenate(backs, axis=1)), 4, axis=1)]

    part = nt(loads[0], w).astype(BF16)
    take = lambda v, i: lax.dynamic_slice_in_dim(v, (i % NX) * quart, quart, 1)
    sent = [lax.ppermute(take(part, x + d), "x", ring(NX, d)) for d in (1, 2, 3)]
    mine = sum(v.astype(F32) for v in [take(part, x)] + sent).astype(BF16)
    scores = in_order([mine] + [from_x(mine, d) for d in (1, 2, 3)], x)
    scores = scores.transpose(1, 0, 2).reshape(k, pix).astype(F32)
    rows = [nt(a, b) for a, b in zip(anchor_ws, loads)]
    rows = pair_sum(rows[0], rows[2], rows[1], rows[3])
    small = nt(rows, rows, precision=HIGHEST)
    lower = jnp.linalg.cholesky(small)
    mix = tri_solve(lower, tri_solve(lower, rows), transpose_a=True)
    abundance = jnp.dot(mix, scores, precision=HIGHEST)
    return (scores, abundance)


def solution(mesh):
    fine = Mesh(mesh.devices.reshape(NZ, NY, NC, NX), ("z", "y", "core", "x"))
    pix = ("z", "y", "core")
    return jax.shard_map(
        local,
        mesh=fine,
        in_specs=(P(pix, "x"), P(None, "x"), P()),
        out_specs=(P(None, pix), P(None, pix)),
        check_vma=False,
    )
```

```python
import jax
import jax.numpy as jnp
from jax import lax
from jax.experimental import pallas as pl
from jax.experimental.pallas import tpu as pltpu
from jax.sharding import Mesh, PartitionSpec as P

ITERS = 5
NZ, NY, NC, NX = 8, 4, 2, 4
F32, BF16 = jnp.float32, jnp.bfloat16
HIGHEST = lax.Precision.HIGHEST


def ring(n, step):
    return [(i, (i + step) % n) for i in range(n)]


def from_x(v, d):
    return lax.ppermute(v, "x", ring(NX, -d))


def tn(a, b):
    return lax.dot_general(a, b, (((0,), (0,)), ((), ())), preferred_element_type=F32)


def nt(a, b, **kw):
    return lax.dot_general(a, b, (((1,), (1,)), ((), ())), preferred_element_type=F32, **kw)


def pair_sum(a, b, c, d):
    return (a + b) + (c + d)


def weigh(block, rowsum, colsum, total):
    expect = rowsum[:, None] * colsum[None, :] / total
    return ((block.astype(F32) - expect) * lax.rsqrt(expect)).astype(BF16)


def eliminate(m, n, full, panel=4):
    lanes = m.shape[1]
    blocks = [m[8 * i:8 * i + 8] for i in range(n // 8)]
    sub = lax.broadcasted_iota(jnp.int32, (8, lanes), 0)
    for k in range(0, n, panel):
        live = range(0 if full else k // 8, n // 8)
        cols = [
            {i: jnp.broadcast_to(blocks[i][:, k + j:k + j + 1], (8, lanes)) for i in live}
            for j in range(panel)
        ]
        for j in range(panel):
            b, r = divmod(k + j, 8)
            inverse = 1.0 / cols[j][b][r:r + 1]
            pivot = blocks[b][r:r + 1] * inverse
            rows = [c[b][r:r + 1] * inverse for c in cols[j + 1:]]
            for i in live:
                if not full and i < b:
                    continue
                factor = cols[j][i]
                if i == b:
                    factor = jnp.where(sub != r if full else sub > r, factor, 0.0)
                blocks[i] = blocks[i] - factor * pivot
                for c, row in zip(cols[j + 1:], rows):
                    c[i] = c[i] - factor * row
    return blocks


def lane_pick(blocks):
    lanes = blocks[0].shape[1]
    lane = lax.broadcasted_iota(jnp.int32, (8, lanes), 1)
    sub = lax.broadcasted_iota(jnp.int32, (8, lanes), 0)
    return [
        jnp.sum(jnp.where(lane == sub + 8 * i, v, 0.0), axis=1, keepdims=True)
        for i, v in enumerate(blocks)
    ]


def factor_body(b0, b1, b2, b3, out, wide):
    k = b0.shape[0]
    backs = [b0[...], b1[...], b2[...], b3[...]]
    grams = [nt(b, b, precision=HIGHEST) for b in backs]
    gram = pair_sum(grams[0], grams[2], grams[1], grams[3])
    eye = lax.broadcasted_iota(jnp.int32, (k, k), 0) == lax.broadcasted_iota(jnp.int32, (k, k), 1)
    wide[:, :k] = gram
    wide[:, k:2 * k] = eye.astype(F32)
    blocks = eliminate(wide[...], k, False)
    blocks = [v * lax.rsqrt(d) for v, d in zip(blocks, lane_pick(blocks))]
    wide[...] = jnp.concatenate(blocks)
    inverse = wide[:, k:2 * k]
    grp = b0.shape[1]
    for i, b in enumerate(backs):
        piece = jnp.dot(inverse, b, precision=HIGHEST, preferred_element_type=F32)
        out[:, i * grp:(i + 1) * grp] = piece.astype(BF16)


def orthonormal(backs):
    k, grp = backs[0].shape
    return pl.pallas_call(
        factor_body,
        out_shape=jax.ShapeDtypeStruct((k, 4 * grp), BF16),
        scratch_shapes=[pltpu.VMEM((k, 2 * k), F32)],
        name="orthonormal",
    )(*backs)


def mix_body(l_ref, a0, a1, a2, a3, out, wide):
    k = l_ref.shape[0]
    na, grp = a0.shape
    rows = [nt(a[...], l_ref[:, i * grp:(i + 1) * grp]) for i, a in enumerate((a0, a1, a2, a3))]
    rows = pair_sum(rows[0], rows[2], rows[1], rows[3])
    wide[...] = jnp.zeros_like(wide)
    wide[:, :na] = nt(rows, rows, precision=HIGHEST)
    wide[:, 128:128 + k] = rows
    blocks = eliminate(wide[...], na, True)
    blocks = [v / d for v, d in zip(blocks, lane_pick(blocks))]
    wide[...] = jnp.concatenate(blocks)
    out[...] = wide[:, 128:128 + k]


def mixing(loads, anchor_ws):
    k, na = loads.shape[0], anchor_ws[0].shape[0]
    return pl.pallas_call(
        mix_body,
        out_shape=jax.ShapeDtypeStruct((na, k), F32),
        scratch_shapes=[pltpu.VMEM((na, 256), F32)],
        name="mixing",
    )(loads, *anchor_ws)


def in_order(parts, me):
    n = len(parts)
    twice = jnp.stack(parts + parts[:-1])
    return lax.dynamic_slice_in_dim(twice, (n - me) % n, n, 0)


def local(spectra, start, anchors):
    pix, grp = spectra.shape
    k = start.shape[0]
    na = anchors.shape[0]
    x, core, y, z = (lax.axis_index(a) for a in ("x", "core", "y", "z"))
    quart = pix // NX

    def quarter(v, j):
        return lax.dynamic_slice_in_dim(v, ((j + 2 * NX) % NX) * quart, quart, 0)

    first = core == 0
    two = lambda v, j: jnp.concatenate([quarter(v, j - 1), quarter(v, j)])
    up = lax.ppermute(two(spectra, x - 1), "x", ring(NX, -1))
    dn = lax.ppermute(two(spectra, x + 1), "x", ring(NX, 1))
    pairs = [(i, (i - 1) % NX) for i in range(NX)] + [(NX + i, NX + (i + 1) % NX) for i in range(NX)]
    extra = lax.ppermute(quarter(spectra, jnp.where(first, x + 1, x + 2)), ("core", "x"), pairs)

    col_part = jnp.sum(spectra, axis=0, dtype=F32)
    row_part = jnp.sum(spectra, axis=1, dtype=F32)
    rowsum = pair_sum(row_part, from_x(row_part, 2), from_x(row_part, 1), from_x(row_part, 3))
    offset = ((z * NY + y) * NC + core) * pix
    positions = lax.broadcasted_iota(jnp.int32, (na, pix), 1)
    picks = anchors[:, None] - offset == positions
    picked = jnp.dot(picks.astype(BF16), spectra, preferred_element_type=F32)
    picked_rows = jnp.sum(jnp.where(picks, row_part[None, :], 0.0), axis=1)
    npix = NZ * NY * NC
    flat = jnp.concatenate([col_part, picked.reshape(na * grp), picked_rows])
    size = -(-flat.shape[0] // (128 * npix)) * 128
    flat = jnp.pad(flat, (0, npix * size - flat.shape[0])).reshape(npix, size)
    over = ("z", "y", "core")
    share = jnp.sum(lax.all_to_all(flat, over, 0, 0, tiled=True), axis=0)
    flat = lax.all_to_all(jnp.broadcast_to(share[None], (npix, size)), over, 0, 0, tiled=True)
    flat = flat.reshape(npix * size)[:(na + 1) * grp + na]
    flats = [flat] + [from_x(flat, d) for d in (1, 2, 3)]
    col = [v[:grp] for v in flats]
    sums = [jnp.sum(v) for v in col]
    total = pair_sum(sums[0], sums[2], sums[1], sums[3])
    sums = [v[(na + 1) * grp:] for v in flats]
    anchor_sum = pair_sum(sums[0], sums[2], sums[1], sums[3])
    anchor_ws = [weigh(v[grp:(na + 1) * grp].reshape(na, grp), anchor_sum, u, total) for u, v in zip(col, flats)]

    w = weigh(spectra, rowsum, col[0], total)
    w_up = weigh(up, two(rowsum, x), col[1], total)
    w_dn = weigh(dn, two(rowsum, x), col[3], total)
    j_extra = jnp.where(first, x - 2, x + 1)
    w_ex = weigh(extra, quarter(rowsum, j_extra), jnp.where(first, col[1], col[3]), total)

    own_a, own_ex = quarter(w, x - 1), quarter(w, j_extra)
    g_own = tn(w, w)
    g_up = tn(own_a, w_up[:quart])
    g_dn = tn(w_dn, two(w, x))
    swap = (x == 0) | (x == 3)
    g_op = tn(jnp.where(swap, w_up, w_dn), jnp.where(swap, w_dn, w_up))
    g_ex = tn(jnp.where(first, own_ex, w_ex), jnp.where(first, w_ex, own_ex))
    g_up = g_up + jnp.where(first, g_ex, 0.0)
    g_dn = g_dn + jnp.where(first, 0.0, g_ex)
    g = jnp.stack([g_own, g_up, g_dn, g_op])

    n1, n2, n3 = grp // NC, grp // NC // NY, grp // npix
    take = lambda v, i, n: lax.dynamic_slice_in_dim(v, i * n, n, 1)
    g = take(g, core, n1) + lax.ppermute(take(g, 1 - core, n1), "core", ring(NC, 1))
    sent = [lax.ppermute(take(g, (y + d) % NY, n2), "y", ring(NY, d)) for d in (1, 2, 3)]
    g = take(g, y, n2) + sent[0] + sent[1] + sent[2]
    g = g.reshape(4, NZ, n3, grp).transpose(1, 0, 2, 3)
    g = jnp.sum(lax.all_to_all(g, "z", 0, 0, tiled=True), axis=0)
    below = lax.ppermute(jnp.stack([g[1], g[3]]), "x", ring(NX, 1))
    above = lax.ppermute(jnp.stack([g[2], g[3]]), "x", ring(NX, -1))
    g = jnp.stack([g[0], g[1] + above[0], g[2] + below[0], below[1] + above[1]])
    g = lax.all_to_all(jnp.broadcast_to(g[None], (NZ,) + g.shape), "z", 0, 0, tiled=True)
    g = in_order([g] + [lax.ppermute(g, "y", ring(NY, -d)) for d in (1, 2, 3)], y)
    g = in_order([g, lax.ppermute(g, "core", ring(NC, 1))], core)
    g = g.transpose(3, 0, 1, 2, 4, 5).reshape(4, grp, grp)
    opposite = jnp.where(x < 2, g[3].T, g[3])
    g = jnp.concatenate([g[0], g[1].T, opposite, g[2]])
    rounded = lax.reduce_precision(g, 8, 7)
    g_hi, g_lo = rounded.astype(BF16), (g - rounded).astype(BF16)

    loads = [start] + [from_x(start, d) for d in (1, 2, 3)]
    whole = jnp.concatenate(loads, axis=1)
    for step in range(ITERS):
        back = jnp.dot(whole, g_hi, preferred_element_type=F32) + jnp.dot(whole, g_lo, preferred_element_type=F32)
        whole = orthonormal([back] + [from_x(back, d) for d in (1, 2, 3)])

    part = nt(whole[:, :grp], w).astype(BF16)
    take = lambda v, i: lax.dynamic_slice_in_dim(v, (i % NX) * quart, quart, 1)
    sent = [lax.ppermute(take(part, x + d), "x", ring(NX, d)) for d in (1, 2, 3)]
    mine = sum(v.astype(F32) for v in [take(part, x)] + sent).astype(BF16)
    scores = in_order([mine] + [from_x(mine, d) for d in (1, 2, 3)], x)
    scores = scores.transpose(1, 0, 2).reshape(k, pix).astype(F32)
    mix = mixing(whole, anchor_ws)
    abundance = jnp.dot(mix, scores, precision=HIGHEST)
    return (scores, abundance)


def solution(mesh):
    fine = Mesh(mesh.devices.reshape(NZ, NY, NC, NX), ("z", "y", "core", "x"))
    pix = ("z", "y", "core")
    return jax.shard_map(
        local,
        mesh=fine,
        in_specs=(P(pix, "x"), P(None, "x"), P()),
        out_specs=(P(None, pix), P(None, pix)),
        check_vma=False,
    )
```

```python
import jax
import jax.numpy as jnp
from jax import lax
from jax.experimental import pallas as pl
from jax.experimental.pallas import tpu as pltpu
from jax.sharding import Mesh, PartitionSpec as P

ITERS = 5
NZ, NY, NC, NX = 8, 4, 2, 4
F32, BF16 = jnp.float32, jnp.bfloat16
HIGHEST = lax.Precision.HIGHEST


def ring(n, step):
    return [(i, (i + step) % n) for i in range(n)]


def from_x(v, d):
    return lax.ppermute(v, "x", ring(NX, -d))


def tn(a, b):
    return lax.dot_general(a, b, (((0,), (0,)), ((), ())), preferred_element_type=F32)


def nt(a, b, **kw):
    return lax.dot_general(a, b, (((1,), (1,)), ((), ())), preferred_element_type=F32, **kw)


def pair_sum(a, b, c, d):
    return (a + b) + (c + d)


def weigh(block, rowsum, colsum, total):
    expect = rowsum[:, None] * colsum[None, :] / total
    return ((block.astype(F32) - expect) * lax.rsqrt(expect)).astype(BF16)


def eliminate(m, n, full, panel=4):
    lanes = m.shape[1]
    blocks = [m[8 * i:8 * i + 8] for i in range(n // 8)]
    sub = lax.broadcasted_iota(jnp.int32, (8, lanes), 0)
    for k in range(0, n, panel):
        live = range(0 if full else k // 8, n // 8)
        cols = [
            {i: jnp.broadcast_to(blocks[i][:, k + j:k + j + 1], (8, lanes)) for i in live}
            for j in range(panel)
        ]
        for j in range(panel):
            b, r = divmod(k + j, 8)
            inverse = 1.0 / cols[j][b][r:r + 1]
            pivot = blocks[b][r:r + 1] * inverse
            rows = [c[b][r:r + 1] * inverse for c in cols[j + 1:]]
            for i in live:
                if not full and i < b:
                    continue
                factor = cols[j][i]
                if i == b:
                    factor = jnp.where(sub != r if full else sub > r, factor, 0.0)
                blocks[i] = blocks[i] - factor * pivot
                for c, row in zip(cols[j + 1:], rows):
                    c[i] = c[i] - factor * row
    return blocks


def lane_pick(blocks):
    lanes = blocks[0].shape[1]
    lane = lax.broadcasted_iota(jnp.int32, (8, lanes), 1)
    sub = lax.broadcasted_iota(jnp.int32, (8, lanes), 0)
    return [
        jnp.sum(jnp.where(lane == sub + 8 * i, v, 0.0), axis=1, keepdims=True)
        for i, v in enumerate(blocks)
    ]


def loadings_of(backs, wide, out):
    k, grp = backs[0].shape
    grams = [nt(b, b, precision=HIGHEST) for b in backs]
    gram = pair_sum(grams[0], grams[2], grams[1], grams[3])
    eye = lax.broadcasted_iota(jnp.int32, (k, k), 0) == lax.broadcasted_iota(jnp.int32, (k, k), 1)
    wide[:, :k] = gram
    wide[:, k:2 * k] = eye.astype(F32)
    blocks = eliminate(wide[...], k, False)
    blocks = [v * lax.rsqrt(d) for v, d in zip(blocks, lane_pick(blocks))]
    wide[...] = jnp.concatenate(blocks)
    inverse = wide[:, k:2 * k]
    for i, b in enumerate(backs):
        piece = jnp.dot(inverse, b, precision=HIGHEST, preferred_element_type=F32)
        out[:, i * grp:(i + 1) * grp] = piece.astype(BF16)


def last_body(b0, b1, b2, b3, out, wide):
    loadings_of([b0[...], b1[...], b2[...], b3[...]], wide, out)


def step_body(b0, b1, b2, b3, hi, lo, out, wide, loads, g_hi, g_lo, sems):
    copies = [pltpu.make_async_copy(hi, g_hi, sems.at[0]), pltpu.make_async_copy(lo, g_lo, sems.at[1])]
    for c in copies:
        c.start()
    loadings_of([b0[...], b1[...], b2[...], b3[...]], wide, loads)
    for c in copies:
        c.wait()
    out[...] = jnp.dot(loads[...], g_hi[...], preferred_element_type=F32) + jnp.dot(
        loads[...], g_lo[...], preferred_element_type=F32
    )


def orthonormal(backs):
    k, grp = backs[0].shape
    return pl.pallas_call(
        last_body,
        out_shape=jax.ShapeDtypeStruct((k, 4 * grp), BF16),
        scratch_shapes=[pltpu.VMEM((k, 2 * k), F32)],
        name="orthonormal",
    )(*backs)


def iterate(backs, g_hi, g_lo):
    k, grp = backs[0].shape
    vmem, whole = pl.BlockSpec(memory_space=pltpu.VMEM), pl.BlockSpec(memory_space=pl.ANY)
    return pl.pallas_call(
        step_body,
        out_shape=jax.ShapeDtypeStruct((k, grp), F32),
        in_specs=[vmem] * 4 + [whole] * 2,
        out_specs=vmem,
        scratch_shapes=[
            pltpu.VMEM((k, 2 * k), F32),
            pltpu.VMEM((k, 4 * grp), BF16),
            pltpu.VMEM((4 * grp, grp), BF16),
            pltpu.VMEM((4 * grp, grp), BF16),
            pltpu.SemaphoreType.DMA((2,)),
        ],
        name="iterate",
    )(*backs, g_hi, g_lo)


def mix_body(l_ref, a0, a1, a2, a3, out, wide):
    k = l_ref.shape[0]
    na, grp = a0.shape
    rows = [nt(a[...], l_ref[:, i * grp:(i + 1) * grp]) for i, a in enumerate((a0, a1, a2, a3))]
    rows = pair_sum(rows[0], rows[2], rows[1], rows[3])
    wide[...] = jnp.zeros_like(wide)
    wide[:, :na] = nt(rows, rows, precision=HIGHEST)
    wide[:, 128:128 + k] = rows
    blocks = eliminate(wide[...], na, True)
    blocks = [v / d for v, d in zip(blocks, lane_pick(blocks))]
    wide[...] = jnp.concatenate(blocks)
    out[...] = wide[:, 128:128 + k]


def mixing(loads, anchor_ws):
    k, na = loads.shape[0], anchor_ws[0].shape[0]
    return pl.pallas_call(
        mix_body,
        out_shape=jax.ShapeDtypeStruct((na, k), F32),
        scratch_shapes=[pltpu.VMEM((na, 256), F32)],
        name="mixing",
    )(loads, *anchor_ws)


def in_order(parts, me):
    n = len(parts)
    twice = jnp.stack(parts + parts[:-1])
    return lax.dynamic_slice_in_dim(twice, (n - me) % n, n, 0)


def local(spectra, start, anchors):
    pix, grp = spectra.shape
    k = start.shape[0]
    na = anchors.shape[0]
    x, core, y, z = (lax.axis_index(a) for a in ("x", "core", "y", "z"))
    quart = pix // NX

    def quarter(v, j):
        return lax.dynamic_slice_in_dim(v, ((j + 2 * NX) % NX) * quart, quart, 0)

    first = core == 0
    two = lambda v, j: jnp.concatenate([quarter(v, j - 1), quarter(v, j)])
    up = lax.ppermute(two(spectra, x - 1), "x", ring(NX, -1))
    dn = lax.ppermute(two(spectra, x + 1), "x", ring(NX, 1))
    pairs = [(i, (i - 1) % NX) for i in range(NX)] + [(NX + i, NX + (i + 1) % NX) for i in range(NX)]
    extra = lax.ppermute(quarter(spectra, jnp.where(first, x + 1, x + 2)), ("core", "x"), pairs)

    col_part = jnp.sum(spectra, axis=0, dtype=F32)
    row_part = jnp.sum(spectra, axis=1, dtype=F32)
    offset = ((z * NY + y) * NC + core) * pix
    positions = lax.broadcasted_iota(jnp.int32, (na, pix), 1)
    picks = anchors[:, None] - offset == positions
    picked = jnp.dot(picks.astype(BF16), spectra, preferred_element_type=F32)
    picked_rows = jnp.sum(jnp.where(picks, row_part[None, :], 0.0), axis=1)
    flat = jnp.concatenate([col_part, picked.reshape(na * grp), picked_rows, row_part])
    flats = [flat] + [from_x(flat, d) for d in (1, 2, 3)]
    cut = (na + 1) * grp
    parts = [v[cut:] for v in flats]
    parts = pair_sum(parts[0], parts[2], parts[1], parts[3])
    rowsum = parts[na:]
    npix = NZ * NY * NC
    flat = jnp.concatenate([v[:cut] for v in flats] + [parts[:na]])
    size = -(-flat.shape[0] // (128 * npix)) * 128
    flat = jnp.pad(flat, (0, npix * size - flat.shape[0])).reshape(npix, size)
    over = ("z", "y", "core")
    share = jnp.sum(lax.all_to_all(flat, over, 0, 0, tiled=True), axis=0)
    flat = lax.all_to_all(jnp.broadcast_to(share[None], (npix, size)), over, 0, 0, tiled=True)
    flat = flat.reshape(npix * size)
    flats = [flat[i * cut:(i + 1) * cut] for i in range(NX)]
    col = [v[:grp] for v in flats]
    sums = [jnp.sum(v) for v in col]
    total = pair_sum(sums[0], sums[2], sums[1], sums[3])
    anchor_sum = flat[NX * cut:NX * cut + na]
    anchor_ws = [weigh(v[grp:].reshape(na, grp), anchor_sum, u, total) for u, v in zip(col, flats)]

    w = weigh(spectra, rowsum, col[0], total)
    n1, n2, n3 = grp // NC, grp // NC // NY, grp // npix
    take = lambda v, i, n: lax.dynamic_slice_in_dim(v, i * n, n, 1)

    def reduced(g):
        g = take(g, core, n1) + lax.ppermute(take(g, 1 - core, n1), "core", ring(NC, 1))
        sent = [lax.ppermute(take(g, (y + d) % NY, n2), "y", ring(NY, d)) for d in (1, 2, 3)]
        g = take(g, y, n2) + sent[0] + sent[1] + sent[2]
        g = g.reshape(g.shape[0], NZ, n3, grp).transpose(1, 0, 2, 3)
        return jnp.sum(lax.all_to_all(g, "z", 0, 0, tiled=True), axis=0)

    def gathered(g):
        g = lax.all_to_all(jnp.broadcast_to(g[None], (NZ,) + g.shape), "z", 0, 0, tiled=True)
        g = in_order([g] + [lax.ppermute(g, "y", ring(NY, -d)) for d in (1, 2, 3)], y)
        g = in_order([g, lax.ppermute(g, "core", ring(NC, 1))], core)
        return g.transpose(3, 0, 1, 2, 4, 5).reshape(g.shape[3], grp, grp)

    own = reduced(tn(w, w)[None])
    up, dn, extra, own = lax.optimization_barrier((up, dn, extra, own))
    w_up = weigh(up, two(rowsum, x), col[1], total)
    w_dn = weigh(dn, two(rowsum, x), col[3], total)
    j_extra = jnp.where(first, x - 2, x + 1)
    w_ex = weigh(extra, quarter(rowsum, j_extra), jnp.where(first, col[1], col[3]), total)

    own_a, own_ex = quarter(w, x - 1), quarter(w, j_extra)
    g_up = tn(own_a, w_up[:quart])
    g_dn = tn(w_dn, two(w, x))
    swap = (x == 0) | (x == 3)
    g_op = tn(jnp.where(swap, w_up, w_dn), jnp.where(swap, w_dn, w_up))
    g_ex = tn(jnp.where(first, own_ex, w_ex), jnp.where(first, w_ex, own_ex))
    g_up = g_up + jnp.where(first, g_ex, 0.0)
    g_dn = g_dn + jnp.where(first, 0.0, g_ex)

    g_own = gathered(own)[0]
    g = reduced(jnp.stack([g_up, g_dn, g_op]))
    below = lax.ppermute(jnp.stack([g[0], g[2]]), "x", ring(NX, 1))
    above = lax.ppermute(jnp.stack([g[1], g[2]]), "x", ring(NX, -1))
    g = gathered(jnp.stack([g[0] + above[0], g[1] + below[0], below[1] + above[1]]))
    opposite = jnp.where(x < 2, g[2].T, g[2])
    g = jnp.concatenate([g_own, g[0].T, opposite, g[1]])
    rounded = lax.reduce_precision(g, 8, 7)
    g_hi, g_lo = rounded.astype(BF16), (g - rounded).astype(BF16)

    loads = [start] + [from_x(start, d) for d in (1, 2, 3)]
    whole = jnp.concatenate(loads, axis=1)
    back = jnp.dot(whole, g_hi, preferred_element_type=F32) + jnp.dot(whole, g_lo, preferred_element_type=F32)
    exchanged = lambda v: [v] + [from_x(v, d) for d in (1, 2, 3)]
    back = lax.fori_loop(0, ITERS - 1, lambda _, v: iterate(exchanged(v), g_hi, g_lo), back)
    whole = orthonormal(exchanged(back))

    part = nt(whole[:, :grp], w).astype(BF16)
    take = lambda v, i: lax.dynamic_slice_in_dim(v, (i % NX) * quart, quart, 1)
    sent = [lax.ppermute(take(part, x + d), "x", ring(NX, d)) for d in (1, 2, 3)]
    mine = sum(v.astype(F32) for v in [take(part, x)] + sent).astype(BF16)
    scores = in_order([mine] + [from_x(mine, d) for d in (1, 2, 3)], x)
    scores = scores.transpose(1, 0, 2).reshape(k, pix).astype(F32)
    mix = mixing(whole, anchor_ws)
    abundance = jnp.dot(mix, scores, precision=HIGHEST)
    return (scores, abundance)


def solution(mesh):
    fine = Mesh(mesh.devices.reshape(NZ, NY, NC, NX), ("z", "y", "core", "x"))
    pix = ("z", "y", "core")
    return jax.shard_map(
        local,
        mesh=fine,
        in_specs=(P(pix, "x"), P(None, "x"), P()),
        out_specs=(P(None, pix), P(None, pix)),
        check_vma=False,
    )
```

```python
import jax
import jax.numpy as jnp
from jax import lax
from jax.experimental import pallas as pl
from jax.experimental.pallas import tpu as pltpu
from jax.sharding import Mesh, PartitionSpec as P

ITERS = 5
NZ, NY, NC, NX = 8, 4, 2, 4
F32, BF16 = jnp.float32, jnp.bfloat16
HIGHEST = lax.Precision.HIGHEST


def ring(n, step):
    return [(i, (i + step) % n) for i in range(n)]


def from_x(v, d):
    return lax.ppermute(v, "x", ring(NX, -d))


def tn(a, b):
    return lax.dot_general(a, b, (((0,), (0,)), ((), ())), preferred_element_type=F32)


def nt(a, b, **kw):
    return lax.dot_general(a, b, (((1,), (1,)), ((), ())), preferred_element_type=F32, **kw)


def pair_sum(a, b, c, d):
    return (a + b) + (c + d)


def weigh(block, rowsum, colsum, total):
    expect = rowsum[:, None] * colsum[None, :] / total
    return ((block.astype(F32) - expect) * lax.rsqrt(expect)).astype(BF16)


def eliminate(m, n, full, panel=4):
    lanes = m.shape[1]
    blocks = [m[8 * i:8 * i + 8] for i in range(n // 8)]
    sub = lax.broadcasted_iota(jnp.int32, (8, lanes), 0)
    for k in range(0, n, panel):
        live = range(0 if full else k // 8, n // 8)
        cols = [
            {i: jnp.broadcast_to(blocks[i][:, k + j:k + j + 1], (8, lanes)) for i in live}
            for j in range(panel)
        ]
        for j in range(panel):
            b, r = divmod(k + j, 8)
            inverse = 1.0 / cols[j][b][r:r + 1]
            pivot = blocks[b][r:r + 1] * inverse
            rows = [c[b][r:r + 1] * inverse for c in cols[j + 1:]]
            for i in live:
                if not full and i < b:
                    continue
                factor = cols[j][i]
                if i == b:
                    factor = jnp.where(sub != r if full else sub > r, factor, 0.0)
                blocks[i] = blocks[i] - factor * pivot
                for c, row in zip(cols[j + 1:], rows):
                    c[i] = c[i] - factor * row
    return blocks


def lane_pick(blocks):
    lanes = blocks[0].shape[1]
    lane = lax.broadcasted_iota(jnp.int32, (8, lanes), 1)
    sub = lax.broadcasted_iota(jnp.int32, (8, lanes), 0)
    return [
        jnp.sum(jnp.where(lane == sub + 8 * i, v, 0.0), axis=1, keepdims=True)
        for i, v in enumerate(blocks)
    ]


def loadings_of(backs, wide, out):
    k, grp = backs[0].shape
    grams = [nt(b, b, precision=HIGHEST) for b in backs]
    gram = pair_sum(grams[0], grams[2], grams[1], grams[3])
    eye = lax.broadcasted_iota(jnp.int32, (k, k), 0) == lax.broadcasted_iota(jnp.int32, (k, k), 1)
    wide[:, :k] = gram
    wide[:, k:2 * k] = eye.astype(F32)
    blocks = eliminate(wide[...], k, False)
    blocks = [v * lax.rsqrt(d) for v, d in zip(blocks, lane_pick(blocks))]
    wide[...] = jnp.concatenate(blocks)
    inverse = wide[:, k:2 * k]
    for i, b in enumerate(backs):
        piece = jnp.dot(inverse, b, precision=HIGHEST, preferred_element_type=F32)
        out[:, i * grp:(i + 1) * grp] = piece.astype(BF16)


def last_body(b0, b1, b2, b3, out, wide):
    loadings_of([b0[...], b1[...], b2[...], b3[...]], wide, out)


def step_body(b0, b1, b2, b3, hi, lo, out, wide, loads, g_hi, g_lo, sems):
    copies = [pltpu.make_async_copy(hi, g_hi, sems.at[0]), pltpu.make_async_copy(lo, g_lo, sems.at[1])]
    for c in copies:
        c.start()
    loadings_of([b0[...], b1[...], b2[...], b3[...]], wide, loads)
    for c in copies:
        c.wait()
    out[...] = jnp.dot(loads[...], g_hi[...], preferred_element_type=F32) + jnp.dot(
        loads[...], g_lo[...], preferred_element_type=F32
    )


def orthonormal(backs):
    k, grp = backs[0].shape
    return pl.pallas_call(
        last_body,
        out_shape=jax.ShapeDtypeStruct((k, 4 * grp), BF16),
        scratch_shapes=[pltpu.VMEM((k, 2 * k), F32)],
        name="orthonormal",
    )(*backs)


def iterate(backs, g_hi, g_lo):
    k, grp = backs[0].shape
    vmem, whole = pl.BlockSpec(memory_space=pltpu.VMEM), pl.BlockSpec(memory_space=pl.ANY)
    return pl.pallas_call(
        step_body,
        out_shape=jax.ShapeDtypeStruct((k, grp), F32),
        in_specs=[vmem] * 4 + [whole] * 2,
        out_specs=vmem,
        scratch_shapes=[
            pltpu.VMEM((k, 2 * k), F32),
            pltpu.VMEM((k, 4 * grp), BF16),
            pltpu.VMEM((4 * grp, grp), BF16),
            pltpu.VMEM((4 * grp, grp), BF16),
            pltpu.SemaphoreType.DMA((2,)),
        ],
        name="iterate",
    )(*backs, g_hi, g_lo)


def mix_body(l_ref, a0, a1, a2, a3, out, wide):
    k = l_ref.shape[0]
    na, grp = a0.shape
    rows = [nt(a[...], l_ref[:, i * grp:(i + 1) * grp]) for i, a in enumerate((a0, a1, a2, a3))]
    rows = pair_sum(rows[0], rows[2], rows[1], rows[3])
    wide[...] = jnp.zeros_like(wide)
    wide[:, :na] = nt(rows, rows, precision=HIGHEST)
    wide[:, 128:128 + k] = rows
    blocks = eliminate(wide[...], na, True)
    blocks = [v / d for v, d in zip(blocks, lane_pick(blocks))]
    wide[...] = jnp.concatenate(blocks)
    out[...] = wide[:, 128:128 + k]


def mixing(loads, anchor_ws):
    k, na = loads.shape[0], anchor_ws[0].shape[0]
    return pl.pallas_call(
        mix_body,
        out_shape=jax.ShapeDtypeStruct((na, k), F32),
        scratch_shapes=[pltpu.VMEM((na, 256), F32)],
        name="mixing",
    )(loads, *anchor_ws)


def in_order(parts, me):
    n = len(parts)
    twice = jnp.stack(parts + parts[:-1])
    return lax.dynamic_slice_in_dim(twice, (n - me) % n, n, 0)


def local(spectra, start, anchors):
    pix, grp = spectra.shape
    k = start.shape[0]
    na = anchors.shape[0]
    x, core, y, z = (lax.axis_index(a) for a in ("x", "core", "y", "z"))
    quart = pix // NX

    def quarter(v, j):
        return lax.dynamic_slice_in_dim(v, ((j + 2 * NX) % NX) * quart, quart, 0)

    first = core == 0
    two = lambda v, j: jnp.concatenate([quarter(v, j - 1), quarter(v, j)])
    up_a = lax.ppermute(quarter(spectra, x - 2), "x", ring(NX, -1))
    dn_a = lax.ppermute(quarter(spectra, x), "x", ring(NX, 1))
    up_b = lax.ppermute(quarter(spectra, x - 1), "x", ring(NX, -1))
    dn_b = lax.ppermute(quarter(spectra, x + 1), "x", ring(NX, 1))
    pairs = [(i, (i - 1) % NX) for i in range(NX)] + [(NX + i, NX + (i + 1) % NX) for i in range(NX)]
    extra = lax.ppermute(quarter(spectra, jnp.where(first, x + 1, x + 2)), ("core", "x"), pairs)

    col_part = jnp.sum(spectra, axis=0, dtype=F32)
    row_part = jnp.sum(spectra, axis=1, dtype=F32)
    offset = ((z * NY + y) * NC + core) * pix
    positions = lax.broadcasted_iota(jnp.int32, (na, pix), 1)
    picks = anchors[:, None] - offset == positions
    picked = jnp.dot(picks.astype(BF16), spectra, preferred_element_type=F32)
    picked_rows = jnp.sum(jnp.where(picks, row_part[None, :], 0.0), axis=1)
    flat = jnp.concatenate([col_part, picked.reshape(na * grp), picked_rows, row_part])
    flats = [flat] + [from_x(flat, d) for d in (1, 2, 3)]
    cut = (na + 1) * grp
    parts = [v[cut:] for v in flats]
    parts = pair_sum(parts[0], parts[2], parts[1], parts[3])
    rowsum = parts[na:]
    npix = NZ * NY * NC
    flat = jnp.concatenate([v[:cut] for v in flats] + [parts[:na]])
    size = -(-flat.shape[0] // (128 * npix)) * 128
    flat = jnp.pad(flat, (0, npix * size - flat.shape[0])).reshape(npix, size)
    over = ("z", "y", "core")
    share = jnp.sum(lax.all_to_all(flat, over, 0, 0, tiled=True), axis=0)
    share, up_a, dn_a = lax.optimization_barrier((share, up_a, dn_a))
    flat = lax.all_to_all(jnp.broadcast_to(share[None], (npix, size)), over, 0, 0, tiled=True)
    flat = flat.reshape(npix * size)
    flats = [flat[i * cut:(i + 1) * cut] for i in range(NX)]
    col = [v[:grp] for v in flats]
    sums = [jnp.sum(v) for v in col]
    total = pair_sum(sums[0], sums[2], sums[1], sums[3])
    anchor_sum = flat[NX * cut:NX * cut + na]
    anchor_ws = [weigh(v[grp:].reshape(na, grp), anchor_sum, u, total) for u, v in zip(col, flats)]

    w = weigh(spectra, rowsum, col[0], total)
    n1, n2, n3 = grp // NC, grp // NC // NY, grp // npix
    take = lambda v, i, n: lax.dynamic_slice_in_dim(v, i * n, n, 1)

    def reduced(g):
        g = take(g, core, n1) + lax.ppermute(take(g, 1 - core, n1), "core", ring(NC, 1))
        sent = [lax.ppermute(take(g, (y + d) % NY, n2), "y", ring(NY, d)) for d in (1, 2, 3)]
        g = take(g, y, n2) + sent[0] + sent[1] + sent[2]
        return g

    def reduced_z(g):
        g = g.reshape(g.shape[0], NZ, n3, grp).transpose(1, 0, 2, 3)
        return jnp.sum(lax.all_to_all(g, "z", 0, 0, tiled=True), axis=0)

    def gathered(g):
        g = lax.all_to_all(jnp.broadcast_to(g[None], (NZ,) + g.shape), "z", 0, 0, tiled=True)
        g = in_order([g] + [lax.ppermute(g, "y", ring(NY, -d)) for d in (1, 2, 3)], y)
        g = in_order([g, lax.ppermute(g, "core", ring(NC, 1))], core)
        return g.transpose(3, 0, 1, 2, 4, 5).reshape(g.shape[3], grp, grp)

    own = tn(w, w)[None]
    own, up_b, dn_b = lax.optimization_barrier((own, up_b, dn_b))
    own = reduced(own)
    own, extra = lax.optimization_barrier((own, extra))
    own = reduced_z(own)
    up, dn = jnp.concatenate([up_a, up_b]), jnp.concatenate([dn_a, dn_b])
    w_up = weigh(up, two(rowsum, x), col[1], total)
    w_dn = weigh(dn, two(rowsum, x), col[3], total)
    j_extra = jnp.where(first, x - 2, x + 1)
    w_ex = weigh(extra, quarter(rowsum, j_extra), jnp.where(first, col[1], col[3]), total)

    own_a, own_ex = quarter(w, x - 1), quarter(w, j_extra)
    g_up = tn(own_a, w_up[:quart])
    g_dn = tn(w_dn, two(w, x))
    swap = (x == 0) | (x == 3)
    g_op = tn(jnp.where(swap, w_up, w_dn), jnp.where(swap, w_dn, w_up))
    g_ex = tn(jnp.where(first, own_ex, w_ex), jnp.where(first, w_ex, own_ex))
    g_up = g_up + jnp.where(first, g_ex, 0.0)
    g_dn = g_dn + jnp.where(first, 0.0, g_ex)

    g = reduced_z(reduced(jnp.stack([g_up, g_dn, g_op])))
    below = lax.ppermute(jnp.stack([g[0], g[2]]), "x", ring(NX, 1))
    above = lax.ppermute(jnp.stack([g[1], g[2]]), "x", ring(NX, -1))
    g = gathered(jnp.stack([own[0], g[0] + above[0], g[1] + below[0], below[1] + above[1]]))
    opposite = jnp.where(x < 2, g[3].T, g[3])
    g = jnp.concatenate([g[0], g[1].T, opposite, g[2]])
    rounded = lax.reduce_precision(g, 8, 7)
    g_hi, g_lo = rounded.astype(BF16), (g - rounded).astype(BF16)

    loads = [start] + [from_x(start, d) for d in (1, 2, 3)]
    whole = jnp.concatenate(loads, axis=1)
    back = jnp.dot(whole, g_hi, preferred_element_type=F32) + jnp.dot(whole, g_lo, preferred_element_type=F32)
    exchanged = lambda v: [v] + [from_x(v, d) for d in (1, 2, 3)]
    back = lax.fori_loop(0, ITERS - 1, lambda _, v: iterate(exchanged(v), g_hi, g_lo), back)
    whole = orthonormal(exchanged(back))

    part = nt(whole[:, :grp], w).astype(BF16)
    take = lambda v, i: lax.dynamic_slice_in_dim(v, (i % NX) * quart, quart, 1)
    sent = [lax.ppermute(take(part, x + d), "x", ring(NX, d)) for d in (1, 2, 3)]
    mine = sum(v.astype(F32) for v in [take(part, x)] + sent).astype(BF16)
    scores = in_order([mine] + [from_x(mine, d) for d in (1, 2, 3)], x)
    scores = scores.transpose(1, 0, 2).reshape(k, pix).astype(F32)
    mix = mixing(whole, anchor_ws)
    abundance = jnp.dot(mix, scores, precision=HIGHEST)
    return (scores, abundance)


def solution(mesh):
    fine = Mesh(mesh.devices.reshape(NZ, NY, NC, NX), ("z", "y", "core", "x"))
    pix = ("z", "y", "core")
    return jax.shard_map(
        local,
        mesh=fine,
        in_specs=(P(pix, "x"), P(None, "x"), P()),
        out_specs=(P(None, pix), P(None, pix)),
        check_vma=False,
    )
```
